1024 devices in a mesh: dp: 128 (over y_lo, z, x), mp: 8 (over y_hi, core).
Axes of the slice: x: 8, y: 8 (y_hi: 4, y_lo: 2; y = y_hi * 2 + y_lo), z: 8, core: 2. Of those that a mesh axis runs over, the one named last changes fastest.
Arguments:
- query_states: bfloat16 [16384, 8192], P('dp', 'mp'), may hold values from -35.35534 to 35.35534
- key_states: bfloat16 [16384, 1024], P('dp', 'mp'), may hold values from -3 to 3
- value_states: bfloat16 [16384, 1024], P('dp', 'mp'), may hold values from -6 to 6
- grad_context: bfloat16 [16384, 8192], P('dp', 'mp'), may hold values from -6 to 6
- inputs_normed: bfloat16 [16384, 4096], P('dp'), may hold values from -24 to 24
- projections: bfloat16 [2, 4096, 1024], P(None, None, 'mp'), may hold values from -0.09375 to 0.09375
Outputs:
- grad_query: bfloat16 [16384, 8192], P('dp', 'mp')
- grad_input: bfloat16 [16384, 4096], P('dp', 'mp')
- grad_weights: float32 [4096, 1024], P('dp', 'mp')
The draws below stay inside these ranges and needn't reach their ends.
All inputs are finite; a program needn't handle non-finite values.
Results may differ from the reference program's by a relative error of at most 0.013.
Values may be sent and summed in bfloat16 or wider, within the bound.
A program may use at most 32 MiB of HBM per device.

```python
import math
import jax
import jax.numpy as jnp
from jax import lax

D = 4096
HEAD_SIZE = 128
QUERY_HEADS = 64
KEY_VALUE_HEADS = 8
SEQUENCE_TOKENS = 128
QUERY_PER_KEY = 8
QW = 8192
KVW = 1024
TOTAL_TOKENS = 16384
N_DP = 128
N_MP = 8


def joint_draw(key):
    query_key = jax.random.fold_in(key, 101)
    random_key_for_keys = jax.random.fold_in(key, 202)
    queries = jnp.clip(jax.random.normal(query_key, (TOTAL_TOKENS, QUERY_HEADS * HEAD_SIZE), jnp.float32), -3.0, 3.0)
    random_key_list = jnp.clip(jax.random.normal(random_key_for_keys, (TOTAL_TOKENS, KEY_VALUE_HEADS * HEAD_SIZE), jnp.float32), -3.0, 3.0)
    return (queries, random_key_list)


def draw_query_states(key, part):
    return joint_draw(key)[0].astype(jnp.bfloat16)


def draw_key_states(key, part):
    return joint_draw(key)[1].astype(jnp.bfloat16)


def strengthened(array, rng, source, target, parts, factor):
    def block_of(position):
        return (jnp.arange(array.shape[position]) // (array.shape[position] // parts)).reshape((-1,) + (1,) * (array.ndim - 1 - position))

    one_side = jax.random.permutation(rng, parts)[block_of(target)]
    second = (block_of(target) + parts // 2) % parts
    return jnp.where((block_of(source) == one_side) | (block_of(source) == second), factor * array, array)


def block_scale(key, dims, split, least, largest):
    factor_of = 1.0
    for position, blocks in split:
        steps = jax.random.uniform(jax.random.fold_in(jax.random.fold_in(key, 6), position), (blocks,), jnp.float32, least / len(split), largest / len(split))
        factor_of = factor_of * jnp.repeat(jnp.exp(steps), dims[position] // blocks).reshape((-1,) + (1,) * (len(dims) - 1 - position))
    return factor_of


def bell_draw(own_key, extent, scale, most, pieces=(), held_as=jnp.bfloat16):
    factor_of = block_scale(own_key, extent, pieces, -0.22, 0.18) if pieces else 1.0
    drawn = jax.random.normal(own_key, extent, jnp.float32) * scale * factor_of
    return jnp.minimum(jnp.maximum(drawn, -most), most).astype(held_as)


def bell_draw_with(stream_key, extent, deviation, reach, pieces, heavy, kind=jnp.bfloat16):
    values = deviation * jax.random.normal(stream_key, extent, jnp.float32)
    if pieces:
        values = values * block_scale(stream_key, extent, pieces, -0.22, 0.18)
    return jnp.clip(strengthened(values, jax.random.fold_in(stream_key, 3), *heavy), -reach, reach).astype(kind)


def setup_inputs(seed: int = 0) -> dict:
    arg_keys = jax.random.split(jax.random.key(seed), 7)
    query_states = draw_query_states(jax.random.fold_in(arg_keys[6], 71), 0)
    key_states = draw_key_states(jax.random.fold_in(arg_keys[6], 71), 0)
    value_states = bell_draw(arg_keys[2], (TOTAL_TOKENS, KVW), 1.0, 6.0, ((0, 128), (1, 8)))
    grad_context = bell_draw(arg_keys[3], (TOTAL_TOKENS, QW), 1.0, 6.0, ((0, 128), (1, 8)))
    inputs_normed = bell_draw_with(arg_keys[4], (TOTAL_TOKENS, D), 1.0, 24.0, ((0, 128),), (0, 1, 128, 5.5))
    projections = bell_draw(arg_keys[5], (2, D, KVW), D ** -0.5, 0.09375, ((2, 8),))
    return dict(query_states=query_states, key_states=key_states, value_states=value_states, grad_context=grad_context, inputs_normed=inputs_normed, projections=projections)


def sequence_grads(query_token_rows, key_token_rows, value_token_rows, gradient_token_rows):
    scale = 1.0 / math.sqrt(HEAD_SIZE)
    query_per_head = query_token_rows.reshape(SEQUENCE_TOKENS, KEY_VALUE_HEADS, QUERY_PER_KEY, HEAD_SIZE).astype(jnp.float32)
    key_per_head = key_token_rows.reshape(SEQUENCE_TOKENS, KEY_VALUE_HEADS, HEAD_SIZE).astype(jnp.float32)
    value_per_head = value_token_rows.reshape(SEQUENCE_TOKENS, KEY_VALUE_HEADS, HEAD_SIZE).astype(jnp.float32)
    gradient_per_head = gradient_token_rows.reshape(SEQUENCE_TOKENS, KEY_VALUE_HEADS, QUERY_PER_KEY, HEAD_SIZE).astype(jnp.float32)
    scores = jnp.einsum('ikgd,jkd->kgij', query_per_head, key_per_head) * scale
    positions = jnp.arange(SEQUENCE_TOKENS, dtype=jnp.int32)[:, None]
    targets = jnp.arange(SEQUENCE_TOKENS, dtype=jnp.int32)[None, :]
    allowed = targets <= positions
    masked = jnp.where(allowed, scores, -1e+30)
    row_max = lax.optimization_barrier(jnp.max(masked, axis=-1, keepdims=True))
    raw_weights = jnp.where(allowed, jnp.exp(masked - row_max), 0.0)
    probs = raw_weights / lax.optimization_barrier(jnp.sum(raw_weights, axis=-1, keepdims=True))
    probs_low = lax.optimization_barrier(probs.astype(jnp.bfloat16))
    probs_b = probs_low.astype(jnp.float32)
    grad_value = jnp.einsum('kgij,ikgd->jkd', probs_b, gradient_per_head).astype(jnp.bfloat16)
    grad_probs = jnp.einsum('ikgd,jkd->kgij', gradient_per_head, value_per_head)
    delta = lax.optimization_barrier(jnp.sum(probs * grad_probs, axis=-1, keepdims=True))
    scores_low = lax.optimization_barrier((probs * (grad_probs - delta)).astype(jnp.bfloat16))
    grad_scores = scores_low.astype(jnp.float32)
    grad_query = (jnp.einsum('kgij,jkd->ikgd', grad_scores, key_per_head) * scale).astype(jnp.bfloat16)
    grad_key = (jnp.einsum('kgij,ikgd->jkd', grad_scores, query_per_head) * scale).astype(jnp.bfloat16)
    return (grad_query.reshape(SEQUENCE_TOKENS, QW), grad_key.reshape(SEQUENCE_TOKENS, KVW), grad_value.reshape(SEQUENCE_TOKENS, KVW))

def reference(query_states, key_states, value_states, grad_context, inputs_normed, projections):
    weights_wide = projections.astype(jnp.float32)
    weight_blocks = weights_wide.reshape(2, D, N_MP, KVW // N_MP)
    count_seqs = TOTAL_TOKENS // SEQUENCE_TOKENS

    def per_sequence(running, batch):
        query_token_rows, key_token_rows, value_token_rows, gradient_token_rows, normed_rows = batch
        grad_query, grad_key, grad_value = sequence_grads(query_token_rows, key_token_rows, value_token_rows, gradient_token_rows)
        both_grads = jnp.stack([grad_key, grad_value]).astype(jnp.float32)
        grad_blocks = both_grads.reshape(2, SEQUENCE_TOKENS, N_MP, KVW // N_MP)
        block_partial = jnp.einsum('tsmc,tdmc->msd', grad_blocks, weight_blocks)
        block_low = lax.optimization_barrier(block_partial.astype(jnp.bfloat16)).astype(jnp.float32)
        input_rows = lax.optimization_barrier(jnp.sum(block_low, axis=0)).astype(jnp.bfloat16)
        running = running + jnp.einsum('sd,sc->dc', normed_rows.astype(jnp.float32), both_grads[0])
        return (running, (grad_query, input_rows))
    initial = jnp.zeros((D, KVW), jnp.float32)
    batches = (query_states.reshape(count_seqs, SEQUENCE_TOKENS, QW), key_states.reshape(count_seqs, SEQUENCE_TOKENS, KVW), value_states.reshape(count_seqs, SEQUENCE_TOKENS, KVW), grad_context.reshape(count_seqs, SEQUENCE_TOKENS, QW), inputs_normed.reshape(count_seqs, SEQUENCE_TOKENS, D))
    summed, (query_grads, input_grads) = lax.scan(per_sequence, initial, batches)
    return (query_grads.reshape(TOTAL_TOKENS, QW), input_grads.reshape(TOTAL_TOKENS, D), summed / N_DP)
```

```python
import math

import jax
import jax.numpy as jnp
from jax import lax
from jax.experimental import pallas as pl
from jax.experimental.pallas import tpu as pltpu
from jax.sharding import Mesh
from jax.sharding import PartitionSpec as P

MESH = pl.DeviceIdType.MESH
H = 128
DP = ("yl", "z", "x")
MP = ("yh", "c")
F32 = jnp.float32
BF16 = jnp.bfloat16


def nt(a, b):
    return lax.dot_general(a, b, (((1,), (1,)), ((), ())), preferred_element_type=F32)


def tn(a, b):
    return lax.dot_general(a, b, (((0,), (0,)), ((), ())), preferred_element_type=F32)


def kernel(
    q_hbm, k_hbm, v_hbm, g_hbm, xn_hbm, pr_hbm,
    gq_hbm, gi_ref, gw_ref,
    q, k, v, g, xn, pr, pt, dst, gq, both,
    wf, mp_, mm_, rp, rm, s2, r2,
    bpo, bps, bpr, ysend_p, ysend_m, yr_p, yr_m,
    lsem, osem, xs, xr, s2s, s2r, cs, cr, ys, yr,
):
    yl = lax.axis_index("yl")
    z = lax.axis_index("z")
    x = lax.axis_index("x")
    yh = lax.axis_index("yh")
    c = lax.axis_index("c")
    nheads = q.shape[1] // H
    scale = 1.0 / math.sqrt(H)

    loads = [
        pltpu.make_async_copy(src, dst_, lsem.at[n])
        for n, (src, dst_) in enumerate(
            [(k_hbm, k), (q_hbm, q), (v_hbm, v), (g_hbm, g), (xn_hbm, xn), (pr_hbm, pr)]
        )
    ]
    for cp in loads:
        cp.start()

    a = x + c * (z - x)

    def along_a(step):
        return {"x": (x + (1 - c) * step + 8) % 8, "z": (z + c * step + 8) % 8}

    def along_b(step, ystep):
        return {
            "x": (x + c * step) % 8,
            "z": (z + (1 - c) * step) % 8,
            "yl": (yl + ystep) % 2,
        }

    def along_y(step):
        return {"yh": (yh + step + 4) % 4}

    partner = {"c": 1 - c}
    peers = [partner, along_y(1), along_y(-1), along_a(1), along_a(-1)]
    peers += [along_b(n % 8, n // 8) for n in range(1, 16)]
    barrier = pltpu.get_barrier_semaphore()
    for peer in peers:
        pl.semaphore_signal(barrier, inc=1, device_id=peer, device_id_type=MESH)

    jpos = lax.broadcasted_iota(jnp.int32, (H, H), 0)
    ipos = lax.broadcasted_iota(jnp.int32, (H, H), 1)
    allowed = jpos <= ipos
    for n in range(4):
        loads[n].wait()
    kk = k[...]
    vv = v[...]
    for h in range(nheads):
        cols = slice(h * H, (h + 1) * H)
        st = jnp.where(allowed, nt(kk, q[:, cols]), -1e30)
        m = jnp.max(st, axis=0, keepdims=True)
        e = jnp.exp2((st - m) * (scale * math.log2(math.e)))
        p = e * (1.0 / jnp.sum(e, axis=0, keepdims=True))
        pt[:, cols] = p.astype(BF16)
        gp = nt(vv, g[:, cols])
        delta = jnp.sum(p * gp, axis=0, keepdims=True)
        dst[:, cols] = (p * (gp - delta)).astype(BF16)

    def stacked(ref):
        return jnp.concatenate([ref[:, h * H : (h + 1) * H] for h in range(nheads)], axis=0)

    gk = jnp.dot(dst[...], stacked(q), preferred_element_type=F32) * scale
    both[:, :H] = gk.astype(BF16)
    gv = jnp.dot(pt[...], stacked(g), preferred_element_type=F32)
    both[:, H:] = gv.astype(BF16)

    loads[4].wait()
    gkb = both[:, :H]

    @pl.loop(0, 16)
    def _(i):
        lanes = pl.ds(pl.multiple_of(i * 256, 256), 256)
        res = tn(xn[:, lanes], gkb)
        for n in range(8):
            place = n + c * (i % 8 - n)
            slot = i + c * ((i // 8) * 8 + n - i)
            wf[place, slot] = res[n * 32 : (n + 1) * 32]

    pl.semaphore_wait(barrier, len(peers))

    LO, HI = slice(0, 8), slice(8, 16)
    msgs = (mp_, mm_)
    recs = (rp, rm)

    def acopy(d, s, half):
        sl = pl.ds(half * 8, 8)
        return pltpu.make_async_remote_copy(
            src_ref=msgs[d].at[s, sl],
            dst_ref=recs[d].at[s, sl],
            send_sem=xs.at[d, s, half],
            recv_sem=xr.at[d, s, half],
            device_id=along_a(1 - 2 * d),
            device_id_type=MESH,
        )

    acopies = {}

    def asend(d, s, half, merged):
        sl = slice(half * 8, half * 8 + 8)
        target = (a + (1 - 2 * d) * (4 - s) + 8) % 8
        val = wf[target, sl]
        if merged:
            acopies[d, s - 1, half].wait_recv()
            val = val + recs[d][s - 1, sl].astype(F32)
        msgs[d][s, sl] = val.astype(BF16)
        cp = acopy(d, s, half)
        acopies[d, s, half] = cp
        cp.start()

    for d in range(2):
        asend(d, 0, d, False)
    for d in range(2):
        asend(d, 1, 1 - d, False)

    loads[5].wait()
    bb = both[...]

    def partial(yt, core):
        rows = pl.ds(pl.multiple_of((yt * 2 + core) * 512, 512), 512)
        return nt(bb[:, :H], pr[0, rows, :]) + nt(bb[:, H:], pr[1, rows, :])

    ccopies = []
    for n, dy in enumerate((2, 1, 3, 0)):
        bps[n] = partial((yh + dy) % 4, 1 - c).astype(BF16)
        cp = pltpu.make_async_remote_copy(
            src_ref=bps.at[n], dst_ref=bpr.at[n],
            send_sem=cs.at[n], recv_sem=cr.at[n],
            device_id=partner, device_id_type=MESH,
        )
        cp.start()
        ccopies.append(cp)
    for n, dy in enumerate((2, 1, 3, 0)):
        bpo[n] = partial((yh + dy) % 4, c)

    ysrc = (ysend_p, ysend_m)
    yrec = (yr_p, yr_m)
    ycopies = {}

    def ysend(d, piece):
        cp = pltpu.make_async_remote_copy(
            src_ref=ysrc[d].at[piece], dst_ref=yrec[d].at[piece],
            send_sem=ys.at[d, piece], recv_sem=yr.at[d, piece],
            device_id=along_y(1 - 2 * d), device_id_type=MESH,
        )
        ycopies[d, piece] = cp
        cp.start()

    def rows_of(d):
        return slice(d * 64, d * 64 + 64)

    ccopies[0].wait_recv()
    for d in range(2):
        r = rows_of(d)
        ysrc[d][0] = (bpo[0, r] + bpr[0, r].astype(F32)).astype(BF16)
        ysend(d, 0)
    for d in range(2):
        ccopies[1 + d].wait_recv()
        r = rows_of(1 - d)
        ysrc[d][1] = (bpo[1 + d, r] + bpr[1 + d, r].astype(F32)).astype(BF16)
        ysend(d, 1)

    for d in range(2):
        asend(d, 1, d, True)
    for d in range(2):
        asend(d, 2, 1 - d, True)

    def grad_query(hs):
        for h in hs:
            cols = slice(h * H, (h + 1) * H)
            gq[:, cols] = (tn(dst[:, cols], kk) * scale).astype(BF16)

    grad_query(range(0, 4))

    for d in range(2):
        asend(d, 2, d, True)
    for d in range(2):
        asend(d, 3, 1 - d, True)

    for d in range(2):
        ycopies[d, 0].wait_recv()
        r = rows_of(d)
        ysrc[d][2] = (
            bpo[1 + d, r] + bpr[1 + d, r].astype(F32) + yrec[d][0].astype(F32)
        ).astype(BF16)
        ysend(d, 2)

    grad_query(range(4, nheads))
    gq_out = pltpu.make_async_copy(gq, gq_hbm, osem)
    gq_out.start()

    for d in range(2):
        asend(d, 3, d, True)

    for d in range(2):
        for half in range(2):
            acopies[d, 3, half].wait_recv()
    tot = wf[a] + rp[3].astype(F32) + rm[3].astype(F32)
    wf[a] = tot
    s2[...] = tot.astype(BF16)
    b = z + c * (x - z)
    bcopies = []
    for n in range(15, 0, -1):
        slot = ((yl + n // 8) % 2) * 8 + (b + n % 8) % 8
        cp = pltpu.make_async_remote_copy(
            src_ref=s2.at[slot], dst_ref=r2.at[n],
            send_sem=s2s.at[n], recv_sem=s2r.at[n],
            device_id=along_b(n % 8, n // 8), device_id_type=MESH,
        )
        cp.start()
        bcopies.append(cp)

    ccopies[3].wait_recv()
    for d in range(2):
        for piece in (1, 2):
            ycopies[d, piece].wait_recv()
    for r in range(2):
        rr = rows_of(r)
        acc = bpo[3, rr] + bpr[3, rr].astype(F32)
        for d in range(2):
            acc = acc + yrec[d][2 if r == d else 1].astype(F32)
        gi_ref[rr, :] = acc.astype(BF16)

    own = wf[a, yl * 8 + b]
    for cp in bcopies:
        cp.wait_recv()
    for n in range(1, 16):
        own = own + r2[n].astype(F32)
    gw_ref[...] = own * (1.0 / (2 * 8 * 8))

    for cp in list(acopies.values()) + ccopies + list(ycopies.values()) + bcopies:
        cp.wait_send()
    gq_out.wait()


def body(query_states, key_states, value_states, grad_context, inputs_normed, projections):
    t, qw = query_states.shape
    d = inputs_normed.shape[1]
    hbm = pl.BlockSpec(memory_space=pl.ANY)
    vmem = pl.BlockSpec(memory_space=pltpu.VMEM)
    V = pltpu.VMEM
    S = pltpu.SemaphoreType.DMA
    gq, gi, gw = pl.pallas_call(
        kernel,
        out_shape=(
            jax.ShapeDtypeStruct((t, qw), BF16),
            jax.ShapeDtypeStruct((t, d // 8), BF16),
            jax.ShapeDtypeStruct((d // 128, H), F32),
        ),
        in_specs=[hbm] * 6,
        out_specs=(hbm, vmem, vmem),
        scratch_shapes=[
            V((t, qw), BF16), V((t, H), BF16), V((t, H), BF16), V((t, qw), BF16),
            V((t, d), BF16), V((2, d, H), BF16),
            V((t, qw), BF16), V((t, qw), BF16), V((t, qw), BF16), V((t, 2 * H), BF16),
            V((8, 16, 32, H), F32),
            V((4, 16, 32, H), BF16), V((4, 16, 32, H), BF16),
            V((4, 16, 32, H), BF16), V((4, 16, 32, H), BF16),
            V((16, 32, H), BF16), V((16, 32, H), BF16),
            V((4, t, 512), F32), V((4, t, 512), BF16), V((4, t, 512), BF16),
            V((3, t // 2, 512), BF16), V((3, t // 2, 512), BF16),
            V((3, t // 2, 512), BF16), V((3, t // 2, 512), BF16),
            S((6,)), S(()),
            S((2, 4, 2)), S((2, 4, 2)),
            S((16,)), S((16,)),
            S((4,)), S((4,)),
            S((2, 3)), S((2, 3)),
        ],
        compiler_params=pltpu.CompilerParams(collective_id=0, has_side_effects=True),
    )(query_states, key_states, value_states, grad_context, inputs_normed, projections)
    return gq, gi, gw


def solution(mesh):
    torus = Mesh(mesh.devices.reshape(2, 8, 8, 4, 2), DP + MP)
    return jax.shard_map(
        body,
        mesh=torus,
        in_specs=(P(DP, MP), P(DP, MP), P(DP, MP), P(DP, MP), P(DP, None), P(None, None, MP)),
        out_specs=(P(DP, MP), P(DP, MP), P(DP, MP)),
        check_vma=False,
    )
```

```python
import math

import jax
import jax.numpy as jnp
from jax import lax
from jax.experimental import pallas as pl
from jax.experimental.pallas import tpu as pltpu
from jax.sharding import Mesh
from jax.sharding import PartitionSpec as P

MESH = pl.DeviceIdType.MESH
H = 128
DP = ("yl", "z", "x")
MP = ("yh", "c")
F32 = jnp.float32
BF16 = jnp.bfloat16


def nt(a, b):
    return lax.dot_general(a, b, (((1,), (1,)), ((), ())), preferred_element_type=F32)


def tn(a, b):
    return lax.dot_general(a, b, (((0,), (0,)), ((), ())), preferred_element_type=F32)


NCH = 4


def toward(p, q):
    return 0 if q < p or (p == q and q >= 2) else 1


def merges(p, q):
    before = p - 1 if toward(p, q) == 0 else p + 1
    return 0 <= before <= 3 and toward(before, q) == toward(p, q)


def kernel(
    q_hbm, k_hbm, v_hbm, g_hbm, xn_hbm, pr_hbm,
    gq_out, gi_out, gw_out,
    q, k, v, g, xn, pr, pt, dst, gkt, both,
    wt, am, ar, xr, bm, br, fin, s2, r2,
    bpo, bps, bpr, ysend_p, ysend_m, yr_p, yr_m,
    lsem, as_, ars, xrs, bs, brs, s2s, s2r, cs, cr, ys, yr,
):
    yl = lax.axis_index("yl")
    z = lax.axis_index("z")
    x = lax.axis_index("x")
    yh = lax.axis_index("yh")
    c = lax.axis_index("c")
    nheads = q.shape[1] // H
    scale = 1.0 / math.sqrt(H)

    loads = [
        pltpu.make_async_copy(src, dst_, lsem.at[n])
        for n, (src, dst_) in enumerate(
            [(k_hbm, k), (q_hbm, q), (v_hbm, v), (g_hbm, g), (xn_hbm, xn), (pr_hbm, pr)]
        )
    ]
    for cp in loads[:5]:
        cp.start()

    def along_y(step):
        return {"yh": (yh + step + 4) % 4}

    def along_x(n):
        return {"x": (x + n % 8) % 8, "yl": (yl + n // 8) % 2}

    partner = {"c": 1 - c}
    peers = [partner, along_y(1), along_y(-1)]
    peers += [{"z": (z + n) % 8} for n in range(1, 8)]
    peers += [along_x(n) for n in range(1, 16)]
    barrier = pltpu.get_barrier_semaphore()
    for peer in peers:
        pl.semaphore_signal(barrier, inc=1, device_id=peer, device_id_type=MESH)

    def remote(src, dst_, ssem, rsem, device):
        return pltpu.make_async_remote_copy(
            src_ref=src, dst_ref=dst_, send_sem=ssem, recv_sem=rsem,
            device_id=device, device_id_type=MESH,
        )

    jpos = lax.broadcasted_iota(jnp.int32, (H, H), 0)
    ipos = lax.broadcasted_iota(jnp.int32, (H, H), 1)
    allowed = jpos <= ipos
    for n in range(4):
        loads[n].wait()
    loads[5].start()
    kk = k[...]
    vv = v[...]
    for h in range(nheads):
        cols = slice(h * H, (h + 1) * H)
        st = jnp.where(allowed, nt(kk, q[:, cols]), -1e30)
        m = jnp.max(st, axis=0, keepdims=True)
        e = jnp.exp2((st - m) * (scale * math.log2(math.e)))
        p = e * (1.0 / jnp.sum(e, axis=0, keepdims=True))
        pt[:, cols] = p.astype(BF16)
        gp = nt(vv, g[:, cols])
        delta = jnp.sum(p * gp, axis=0, keepdims=True)
        dst[:, cols] = (p * (gp - delta)).astype(BF16)

    def stacked(ref):
        return jnp.concatenate([ref[:, h * H : (h + 1) * H] for h in range(nheads)], axis=0)

    gk = jnp.dot(dst[...], stacked(q), preferred_element_type=F32) * scale
    both[:, :H] = gk.astype(BF16)
    gkt[...] = gk.T.astype(BF16)

    loads[4].wait()
    for t in range(8):
        for half in range(2):
            lanes = slice((half * 8 + t) * 256, (half * 8 + t + 1) * 256)
            wt[t, half] = jnp.dot(gkt[...], xn[:, lanes], preferred_element_type=F32)

    def partials():
        gv = jnp.dot(pt[...], stacked(g), preferred_element_type=F32)
        both[:, H:] = gv.astype(BF16)
        loads[5].wait()
        bb = both[...]

        def partial(yt, core):
            rows = pl.ds(pl.multiple_of((yt * 2 + core) * 512, 512), 512)
            return nt(bb[:, :H], pr[0, rows, :]) + nt(bb[:, H:], pr[1, rows, :])

        for n, dy in enumerate((2, 1, 3, 0)):
            bps[n] = partial((yh + dy) % 4, 1 - c).astype(BF16)
        for n, dy in enumerate((2, 1, 3, 0)):
            bpo[n] = partial((yh + dy) % 4, c)

    def grad_query():
        for h in range(nheads):
            cols = slice(h * H, (h + 1) * H)
            gq_out[:, cols] = (tn(dst[:, cols], kk) * scale).astype(BF16)

    ccopies = [remote(bps.at[n], bpr.at[n], cs.at[n], cr.at[n], partner) for n in range(4)]

    ysrc = (ysend_p, ysend_m)
    yrec = (yr_p, yr_m)
    ycopies = {
        (d, n): remote(ysrc[d].at[n], yrec[d].at[n], ys.at[d, n], yr.at[d, n], along_y(1 - 2 * d))
        for d in range(2)
        for n in range(3)
    }

    def rows_of(d):
        return slice(d * 64, d * 64 + 64)

    def y_swap():
        for cp in ccopies:
            cp.start()

    def y_first():
        ccopies[0].wait_recv()
        for d in range(2):
            r = rows_of(d)
            ysrc[d][0] = (bpo[0, r] + bpr[0, r].astype(F32)).astype(BF16)
            ycopies[d, 0].start()
        for d in range(2):
            ccopies[1 + d].wait_recv()
            r = rows_of(1 - d)
            ysrc[d][1] = (bpo[1 + d, r] + bpr[1 + d, r].astype(F32)).astype(BF16)
            ycopies[d, 1].start()

    def y_second():
        for d in range(2):
            ycopies[d, 0].wait_recv()
            r = rows_of(d)
            ysrc[d][2] = (
                bpo[1 + d, r] + bpr[1 + d, r].astype(F32) + yrec[d][0].astype(F32)
            ).astype(BF16)
            ycopies[d, 2].start()

    def piece(ch):
        return ch // 2, pl.ds(ch % 2 * 64, 64)

    def across(hf, p, qs):
        for q_ in qs:
            d = toward(p, q_)
            last = p == (3 if d == 0 else 0)
            t = 4 * (1 - hf) + q_
            for ch in range(NCH):
                half, rows = piece(ch)
                val = wt[t, half, rows]
                if merges(p, q_):
                    here = ar.at[q_, half, rows]
                    remote(am.at[q_, half, rows], here, as_.at[q_, ch], ars.at[q_, ch], {"z": t}).wait_recv()
                    val = val + ar[q_, half, rows].astype(F32)
                am[q_, half, rows] = val.astype(BF16)
                if last:
                    to, sem, dev = xr.at[d, half, rows], xrs.at[d, ch], t
                else:
                    to, sem, dev = ar.at[q_, half, rows], ars.at[q_, ch], 4 * hf + p + 1 - 2 * d
                remote(am.at[q_, half, rows], to, as_.at[q_, ch], sem, {"z": dev}).start()

    def waits_late(p, q_):
        return toward(p, q_) == 1 and merges(p, q_)

    def within_target(n):
        return z // 4 * 4 + (z % 4 + n) % 4

    bcopies = [
        remote(bm.at[n - 1], br.at[n - 1], bs.at[n - 1], brs.at[n - 1], {"z": within_target(n)})
        for n in range(1, 4)
    ]

    def within():
        for n in range(1, 4):
            bm[n - 1] = wt[within_target(n)].astype(BF16)
            bcopies[n - 1].start()

    @pl.when(z < 4)
    def _():
        partials()
        grad_query()

    pl.semaphore_wait(barrier, len(peers))

    @pl.when(z < 4)
    def _():
        y_swap()
        within()
        for p in range(4):
            pl.when(z == p)(lambda p=p: across(0, p, [n for n in range(4) if not waits_late(p, n)]))
        y_first()
        for p in range(2):
            pl.when(z == p)(lambda p=p: across(0, p, [n for n in range(4) if waits_late(p, n)]))
        y_second()

    @pl.when(z >= 4)
    def _():
        for p in range(4):
            pl.when(z == 4 + p)(lambda p=p: across(1, p, range(4)))
        within()
        partials()
        y_swap()
        grad_query()
        y_first()
        y_second()

    for cp in bcopies:
        cp.wait_recv()
    for d in range(2):
        for ch in range(NCH):
            half, rows = piece(ch)
            remote(
                am.at[0, half, rows], xr.at[d, half, rows], as_.at[0, ch], xrs.at[d, ch], {"z": (z + 1) % 8}
            ).wait_recv()
    for half in range(2):
        tot = wt[z, half] + xr[0, half].astype(F32) + xr[1, half].astype(F32)
        for n in range(3):
            tot = tot + br[n, half].astype(F32)
        tot = tot.T.reshape(8, 32, H)
        fin[half * 8 : half * 8 + 8] = tot
        s2[half * 8 : half * 8 + 8] = tot.astype(BF16)
    scopies = []
    for n in (4, 12, 3, 5, 11, 13, 2, 6, 10, 14, 1, 7, 9, 15, 8):
        slot = (yl + n // 8) % 2 * 8 + (x + n % 8) % 8
        cp = remote(s2.at[slot], r2.at[n], s2s.at[n], s2r.at[n], along_x(n))
        cp.start()
        scopies.append(cp)

    ccopies[3].wait_recv()
    for d in range(2):
        for n in (1, 2):
            ycopies[d, n].wait_recv()
    for r in range(2):
        rr = rows_of(r)
        acc = bpo[3, rr] + bpr[3, rr].astype(F32)
        for d in range(2):
            acc = acc + yrec[d][2 if r == d else 1].astype(F32)
        gi_out[rr, :] = acc.astype(BF16)

    own = fin[yl * 8 + x]
    for cp in scopies:
        cp.wait_recv()
    for n in range(1, 16):
        own = own + r2[n].astype(F32)
    gw_out[...] = own * (1.0 / (2 * 8 * 8))

    for cp in ccopies + list(ycopies.values()) + bcopies + scopies:
        cp.wait_send()
    for q_ in range(4):
        for ch in range(NCH):
            half, rows = piece(ch)
            remote(
                am.at[q_, half, rows], ar.at[q_, half, rows], as_.at[q_, ch], ars.at[q_, ch], {"z": (z + 1) % 8}
            ).wait_send()


def put_out(*refs):
    n = len(refs) // 2
    sem = refs[-1]
    copies = [
        pltpu.make_async_copy(src, dst_, sem.at[i])
        for i, (src, dst_) in enumerate(zip(refs[:n], refs[n : 2 * n]))
    ]
    for cp in copies:
        cp.start()
    for cp in copies:
        cp.wait()


def body(query_states, key_states, value_states, grad_context, inputs_normed, projections):
    t, qw = query_states.shape
    d = inputs_normed.shape[1]
    hbm = pl.BlockSpec(memory_space=pl.ANY)
    vmem = pl.BlockSpec(memory_space=pltpu.VMEM)
    V = pltpu.VMEM
    S = pltpu.SemaphoreType.DMA
    shapes = (
        jax.ShapeDtypeStruct((t, qw), BF16),
        jax.ShapeDtypeStruct((t, d // 8), BF16),
        jax.ShapeDtypeStruct((d // 128, H), F32),
    )
    outs = pl.pallas_call(
        kernel,
        out_shape=tuple(V(s.shape, s.dtype) for s in shapes),
        in_specs=[hbm] * 6,
        out_specs=(vmem,) * 3,
        scratch_shapes=[
            V((t, qw), BF16), V((t, H), BF16), V((t, H), BF16), V((t, qw), BF16),
            V((t, d), BF16), V((2, d, H), BF16),
            V((t, qw), BF16), V((t, qw), BF16), V((H, t), BF16), V((t, 2 * H), BF16),
            V((8, 2, H, 256), F32),
            V((4, 2, H, 256), BF16), V((4, 2, H, 256), BF16), V((2, 2, H, 256), BF16),
            V((3, 2, H, 256), BF16), V((3, 2, H, 256), BF16),
            V((16, 32, H), F32), V((16, 32, H), BF16), V((16, 32, H), BF16),
            V((4, t, 512), F32), V((4, t, 512), BF16), V((4, t, 512), BF16),
            V((3, t // 2, 512), BF16), V((3, t // 2, 512), BF16),
            V((3, t // 2, 512), BF16), V((3, t // 2, 512), BF16),
            S((6,)), S((4, NCH)), S((4, NCH)), S((2, NCH)), S((3,)), S((3,)),
            S((16,)), S((16,)), S((4,)), S((4,)), S((2, 3)), S((2, 3)),
        ],
        compiler_params=pltpu.CompilerParams(collective_id=0, has_side_effects=True),
    )(query_states, key_states, value_states, grad_context, inputs_normed, projections)
    return pl.pallas_call(
        put_out,
        out_shape=shapes,
        in_specs=(vmem,) * 3,
        out_specs=(hbm,) * 3,
        scratch_shapes=[S((3,))],
    )(*[pltpu.with_memory_space_constraint(o, pltpu.VMEM) for o in outs])


def solution(mesh):
    torus = Mesh(mesh.devices.reshape(2, 8, 8, 4, 2), DP + MP)
    return jax.shard_map(
        body,
        mesh=torus,
        in_specs=(P(DP, MP), P(DP, MP), P(DP, MP), P(DP, MP), P(DP, None), P(None, None, MP)),
        out_specs=(P(DP, MP), P(DP, MP), P(DP, MP)),
        check_vma=False,
    )
```

```python
import math

import jax
import jax.numpy as jnp
from jax import lax
from jax.experimental import pallas as pl
from jax.experimental.pallas import tpu as pltpu
from jax.sharding import Mesh
from jax.sharding import PartitionSpec as P

MESH = pl.DeviceIdType.MESH
H = 128
DP = ("yl", "z", "x")
MP = ("yh", "c")
F32 = jnp.float32
BF16 = jnp.bfloat16


def nt(a, b):
    return lax.dot_general(a, b, (((1,), (1,)), ((), ())), preferred_element_type=F32)


def tn(a, b):
    return lax.dot_general(a, b, (((0,), (0,)), ((), ())), preferred_element_type=F32)


NCH = 4


def swap_pieces(tiles):
    lane = lax.broadcasted_iota(jnp.int32, tiles[0].shape, 1)
    for far, width in ((2, 64), (1, 32)):
        low = lane // width % 2 == 0
        out = list(tiles)
        for i in range(4):
            if i // far % 2 == 0:
                p, q = tiles[i], tiles[i + far]
                out[i] = jnp.where(low, p, pltpu.roll(q, width, 1))
                out[i + far] = jnp.where(low, pltpu.roll(p, H - width, 1), q)
        tiles = out
    return tiles


def kernel(
    q_hbm, k_hbm, v_hbm, g_hbm, xn_hbm, pr_hbm,
    gq_out, gi_out, gw_out,
    q, k, v, g, xn, xp, pr, pt, dst, gkt, both,
    wt, am, ar, fm, fr, fin, s2, r2,
    bpo, bps, bpr, ysend_p, ysend_m, yr_p, yr_m,
    lsem, as_, ars, fs, frs, s2s, s2r, cs, cr, ys, yr,
):
    yl = lax.axis_index("yl")
    z = lax.axis_index("z")
    x = lax.axis_index("x")
    yh = lax.axis_index("yh")
    c = lax.axis_index("c")
    nheads = q.shape[1] // H
    scale = 1.0 / math.sqrt(H)

    loads = [
        pltpu.make_async_copy(src, dst_, lsem.at[n])
        for n, (src, dst_) in enumerate(
            [(k_hbm, k), (q_hbm, q), (v_hbm, v), (g_hbm, g), (xn_hbm, xn), (pr_hbm, pr)]
        )
    ]
    for cp in loads[:5]:
        cp.start()

    def along_y(step):
        return {"yh": (yh + step + 4) % 4}

    a = x + c * (z - x)
    b = z + c * (x - z)

    def along_a(step):
        return {"x": (x + (1 - c) * step + 8) % 8, "z": (z + c * step + 8) % 8}

    def along_b(n):
        return {"x": (x + c * (n % 8)) % 8, "z": (z + (1 - c) * (n % 8)) % 8, "yl": (yl + n // 8) % 2}

    partner = {"c": 1 - c}
    peers = [partner, along_y(1), along_y(-1)]
    peers += [along_a(n) for n in (1, -1, 3, -3)]
    peers += [along_b(n) for n in range(1, 16)]
    barrier = pltpu.get_barrier_semaphore()
    for peer in peers:
        pl.semaphore_signal(barrier, inc=1, device_id=peer, device_id_type=MESH)

    def remote(src, dst_, ssem, rsem, device):
        return pltpu.make_async_remote_copy(
            src_ref=src, dst_ref=dst_, send_sem=ssem, recv_sem=rsem,
            device_id=device, device_id_type=MESH,
        )

    jpos = lax.broadcasted_iota(jnp.int32, (H, H), 0)
    ipos = lax.broadcasted_iota(jnp.int32, (H, H), 1)
    allowed = jpos <= ipos
    for n in range(4):
        loads[n].wait()
    loads[5].start()
    kk = k[...]
    vv = v[...]
    for h in range(nheads):
        cols = slice(h * H, (h + 1) * H)
        st = jnp.where(allowed, nt(kk, q[:, cols]), -1e30)
        m = jnp.max(st, axis=0, keepdims=True)
        e = jnp.exp2((st - m) * (scale * math.log2(math.e)))
        p = e * (1.0 / jnp.sum(e, axis=0, keepdims=True))
        pt[:, cols] = p.astype(BF16)
        gp = nt(vv, g[:, cols])
        delta = jnp.sum(p * gp, axis=0, keepdims=True)
        dst[:, cols] = (p * (gp - delta)).astype(BF16)

    def stacked(ref):
        return jnp.concatenate([ref[:, h * H : (h + 1) * H] for h in range(nheads)], axis=0)

    gk = jnp.dot(dst[...], stacked(q), preferred_element_type=F32) * scale
    both[:, :H] = gk.astype(BF16)
    gkt[...] = gk.T.astype(BF16)

    loads[4].wait()

    @pl.when(c == 0)
    def _():
        for zq in range(4):
            for xh in range(2):
                cols = [((zq * 4 + zr) * 2 + xh) * H for zr in range(4)]
                tiles = swap_pieces([xn[:, i : i + H] for i in cols])
                for xl in range(4):
                    to = ((xh * 4 + xl) * 4 + zq) * H
                    xp[:, to : to + H] = tiles[xl]

    @pl.when(c == 1)
    def _():
        for half in range(2):
            for t in range(8):
                xp[:, (t * 2 + half) * 256 : (t * 2 + half + 1) * 256] = xn[
                    :, (half * 8 + t) * 256 : (half * 8 + t + 1) * 256
                ]

    for t in range(8):
        wt[t] = jnp.dot(gkt[...], xp[:, t * 512 : (t + 1) * 512], preferred_element_type=F32)

    def partials():
        gv = jnp.dot(pt[...], stacked(g), preferred_element_type=F32)
        both[:, H:] = gv.astype(BF16)
        loads[5].wait()
        bb = both[...]

        def partial(yt, core):
            rows = pl.ds(pl.multiple_of((yt * 2 + core) * 512, 512), 512)
            return nt(bb[:, :H], pr[0, rows, :]) + nt(bb[:, H:], pr[1, rows, :])

        for n, dy in enumerate((2, 1, 3, 0)):
            bps[n] = partial((yh + dy) % 4, 1 - c).astype(BF16)
        for n, dy in enumerate((2, 1, 3, 0)):
            bpo[n] = partial((yh + dy) % 4, c)

    def grad_query():
        for h in range(nheads):
            cols = slice(h * H, (h + 1) * H)
            gq_out[:, cols] = (tn(dst[:, cols], kk) * scale).astype(BF16)

    ccopies = [remote(bps.at[n], bpr.at[n], cs.at[n], cr.at[n], partner) for n in range(4)]

    ysrc = (ysend_p, ysend_m)
    yrec = (yr_p, yr_m)
    ycopies = {
        (d, n): remote(ysrc[d].at[n], yrec[d].at[n], ys.at[d, n], yr.at[d, n], along_y(1 - 2 * d))
        for d in range(2)
        for n in range(3)
    }

    def rows_of(d):
        return slice(d * 64, d * 64 + 64)

    def y_swap():
        for cp in ccopies:
            cp.start()

    def y_first():
        ccopies[0].wait_recv()
        for d in range(2):
            r = rows_of(d)
            ysrc[d][0] = (bpo[0, r] + bpr[0, r].astype(F32)).astype(BF16)
            ycopies[d, 0].start()
        for d in range(2):
            ccopies[1 + d].wait_recv()
            r = rows_of(1 - d)
            ysrc[d][1] = (bpo[1 + d, r] + bpr[1 + d, r].astype(F32)).astype(BF16)
            ycopies[d, 1].start()

    def y_second():
        for d in range(2):
            ycopies[d, 0].wait_recv()
            r = rows_of(d)
            ysrc[d][2] = (
                bpo[1 + d, r] + bpr[1 + d, r].astype(F32) + yrec[d][0].astype(F32)
            ).astype(BF16)
            ycopies[d, 2].start()

    acopies = {
        (d, m, ch): remote(
            am.at[d, m, pl.ds(ch * 32, 32)], ar.at[d, m, pl.ds(ch * 32, 32)],
            as_.at[d, m, ch], ars.at[d, m, ch], along_a(1 - 2 * d),
        )
        for d in range(2)
        for m in range(3)
        for ch in range(NCH)
    }
    fcopies = [remote(fm.at[d], fr.at[d], fs.at[d], frs.at[d], along_a(3 - 6 * d)) for d in range(2)]

    def chunks(d):
        return (2, 3, 0, 1) if d == 0 else (0, 1, 2, 3)

    def ring(m, d, ch):
        rows = slice(ch * 32, ch * 32 + 32)
        val = wt[(a + (1 - 2 * d) * (3 - m) + 8) % 8, rows]
        if m:
            acopies[d, m - 1, ch].wait_recv()
            val = val + ar[d, m - 1, rows].astype(F32)
        if m == 2 and ch // 2 == d:
            if ch % 2 == 0:
                fcopies[d].wait_recv()
            val = val + fr[d, ch % 2 * 32 : ch % 2 * 32 + 32].astype(F32)
        am[d, m, rows] = val.astype(BF16)
        acopies[d, m, ch].start()

    def ring_step(m):
        for i in range(NCH):
            for d in range(2):
                ring(m, d, chunks(d)[i])

    def ring_start():
        ring_step(0)
        for d in range(2):
            fm[d] = wt[(a + 4) % 8, d * 64 : d * 64 + 64].astype(BF16)
            fcopies[d].start()

    slots = (4, 12, 3, 5, 11, 13, 2, 6, 10, 14, 1, 7, 9, 15, 8)
    scopies = [
        remote(s2.at[(yl + n // 8) % 2 * 8 + (b + n % 8) % 8], r2.at[n], s2s.at[n], s2r.at[n], along_b(n))
        for n in slots
    ]

    def owners():
        for d in range(2):
            for ch in range(NCH):
                acopies[d, 2, ch].wait_recv()
        for half in range(2):
            cols = slice(half * 256, half * 256 + 256)
            tot = wt[a, :, cols] + ar[0, 2, :, cols].astype(F32) + ar[1, 2, :, cols].astype(F32)
            tot = tot.T.reshape(8, 32, H)
            fin[half * 8 : half * 8 + 8] = tot
            s2[half * 8 : half * 8 + 8] = tot.astype(BF16)
        for cp in scopies:
            cp.start()

    @pl.when(z < 4)
    def _():
        partials()
        grad_query()

    pl.semaphore_wait(barrier, len(peers))
    ring_start()

    @pl.when(z < 4)
    def _():
        y_swap()
        y_first()
        ring_step(1)
        y_second()
        ring_step(2)
        owners()

    @pl.when(z >= 4)
    def _():
        ring_step(1)
        ring_step(2)
        owners()
        partials()
        y_swap()
        grad_query()
        y_first()
        y_second()

    ccopies[3].wait_recv()
    for d in range(2):
        for n in (1, 2):
            ycopies[d, n].wait_recv()
    for r in range(2):
        rr = rows_of(r)
        acc = bpo[3, rr] + bpr[3, rr].astype(F32)
        for d in range(2):
            acc = acc + yrec[d][2 if r == d else 1].astype(F32)
        gi_out[rr, :] = acc.astype(BF16)

    own = fin[yl * 8 + b]
    for cp in scopies:
        cp.wait_recv()
    for n in range(1, 16):
        own = own + r2[n].astype(F32)
    gw_out[...] = own * (1.0 / (2 * 8 * 8))

    for cp in ccopies + list(ycopies.values()) + list(acopies.values()) + fcopies + scopies:
        cp.wait_send()


def put_out(*refs):
    n = len(refs) // 2
    sem = refs[-1]
    copies = [
        pltpu.make_async_copy(src, dst_, sem.at[i])
        for i, (src, dst_) in enumerate(zip(refs[:n], refs[n : 2 * n]))
    ]
    for cp in copies:
        cp.start()
    for cp in copies:
        cp.wait()


def body(query_states, key_states, value_states, grad_context, inputs_normed, projections):
    t, qw = query_states.shape
    d = inputs_normed.shape[1]
    hbm = pl.BlockSpec(memory_space=pl.ANY)
    vmem = pl.BlockSpec(memory_space=pltpu.VMEM)
    V = pltpu.VMEM
    S = pltpu.SemaphoreType.DMA
    shapes = (
        jax.ShapeDtypeStruct((t, qw), BF16),
        jax.ShapeDtypeStruct((t, d // 8), BF16),
        jax.ShapeDtypeStruct((d // 128, H), F32),
    )
    outs = pl.pallas_call(
        kernel,
        out_shape=tuple(V(s.shape, s.dtype) for s in shapes),
        in_specs=[hbm] * 6,
        out_specs=(vmem,) * 3,
        scratch_shapes=[
            V((t, qw), BF16), V((t, H), BF16), V((t, H), BF16), V((t, qw), BF16),
            V((t, d), BF16), V((t, d), BF16), V((2, d, H), BF16),
            V((t, qw), BF16), V((t, qw), BF16), V((H, t), BF16), V((t, 2 * H), BF16),
            V((8, H, 512), F32),
            V((2, 3, H, 512), BF16), V((2, 3, H, 512), BF16),
            V((2, H // 2, 512), BF16), V((2, H // 2, 512), BF16),
            V((16, 32, H), F32), V((16, 32, H), BF16), V((16, 32, H), BF16),
            V((4, t, 512), F32), V((4, t, 512), BF16), V((4, t, 512), BF16),
            V((3, t // 2, 512), BF16), V((3, t // 2, 512), BF16),
            V((3, t // 2, 512), BF16), V((3, t // 2, 512), BF16),
            S((6,)), S((2, 3, NCH)), S((2, 3, NCH)), S((2,)), S((2,)),
            S((16,)), S((16,)), S((4,)), S((4,)), S((2, 3)), S((2, 3)),
        ],
        compiler_params=pltpu.CompilerParams(collective_id=0, has_side_effects=True),
    )(query_states, key_states, value_states, grad_context, inputs_normed, projections)
    return pl.pallas_call(
        put_out,
        out_shape=shapes,
        in_specs=(vmem,) * 3,
        out_specs=(hbm,) * 3,
        scratch_shapes=[S((3,))],
    )(*[pltpu.with_memory_space_constraint(o, pltpu.VMEM) for o in outs])


def solution(mesh):
    torus = Mesh(mesh.devices.reshape(2, 8, 8, 4, 2), DP + MP)
    return jax.shard_map(
        body,
        mesh=torus,
        in_specs=(P(DP, MP), P(DP, MP), P(DP, MP), P(DP, MP), P(DP, None), P(None, None, MP)),
        out_specs=(P(DP, MP), P(DP, MP), P(DP, MP)),
        check_vma=False,
    )
```

```python
import math

import jax
import jax.numpy as jnp
from jax import lax
from jax.experimental import pallas as pl
from jax.experimental.pallas import tpu as pltpu
from jax.sharding import Mesh
from jax.sharding import PartitionSpec as P

MESH = pl.DeviceIdType.MESH
H = 128
DP = ("yl", "z", "x")
MP = ("yh", "c")
F32 = jnp.float32
BF16 = jnp.bfloat16


def nt(a, b):
    return lax.dot_general(a, b, (((1,), (1,)), ((), ())), preferred_element_type=F32)


def tn(a, b):
    return lax.dot_general(a, b, (((0,), (0,)), ((), ())), preferred_element_type=F32)


NCH = 4


def swap_pieces(tiles):
    place = lax.broadcasted_iota(jnp.int32, tiles[0].shape, 1) // 32
    turned = [tiles[0]] + [pltpu.roll(tiles[j], 32 * j, 1) for j in range(1, 4)]
    out = []
    for i in range(4):
        mixed = turned[0]
        for j in range(1, 4):
            mixed = jnp.where(place == (i + j) % 4, turned[j], mixed)
        out.append(pltpu.roll(mixed, H - 32 * i, 1) if i else mixed)
    return out


def kernel(
    q_hbm, k_hbm, v_hbm, g_hbm, xn_hbm, pr_hbm,
    gq_out, gi_out, gw_out,
    q, k, v, g, xn, xp, pr, pt, dst, gkt, both,
    wt, am, ar, fm, fr, fin, s2, r2,
    bpo, bps, bpr, ysend_p, ysend_m, yr_p, yr_m,
    lsem, as_, ars, fs, frs, s2s, s2r, cs, cr, ys, yr,
):
    yl = lax.axis_index("yl")
    z = lax.axis_index("z")
    x = lax.axis_index("x")
    yh = lax.axis_index("yh")
    c = lax.axis_index("c")
    nheads = q.shape[1] // H
    scale = 1.0 / math.sqrt(H)

    loads = [
        pltpu.make_async_copy(src, dst_, lsem.at[n])
        for n, (src, dst_) in enumerate(
            [(k_hbm, k), (q_hbm, q), (v_hbm, v), (g_hbm, g), (xn_hbm, xn), (pr_hbm, pr)]
        )
    ]
    for cp in loads[:5]:
        cp.start()

    def along_y(step):
        return {"yh": (yh + step + 4) % 4}

    a = x + c * (z - x)
    b = z + c * (x - z)

    def along_a(step):
        return {"x": (x + (1 - c) * step + 8) % 8, "z": (z + c * step + 8) % 8}

    def along_b(n):
        return {"x": (x + c * (n % 8)) % 8, "z": (z + (1 - c) * (n % 8)) % 8, "yl": (yl + n // 8) % 2}

    partner = {"c": 1 - c}
    peers = [partner, along_y(1), along_y(-1)]
    peers += [along_a(n) for n in (1, -1, 3, -3)]
    peers += [along_b(n) for n in range(1, 16)]
    barrier = pltpu.get_barrier_semaphore()
    for peer in peers:
        pl.semaphore_signal(barrier, inc=1, device_id=peer, device_id_type=MESH)

    def remote(src, dst_, ssem, rsem, device):
        return pltpu.make_async_remote_copy(
            src_ref=src, dst_ref=dst_, send_sem=ssem, recv_sem=rsem,
            device_id=device, device_id_type=MESH,
        )

    jpos = lax.broadcasted_iota(jnp.int32, (H, H), 0)
    ipos = lax.broadcasted_iota(jnp.int32, (H, H), 1)
    allowed = jpos <= ipos
    for n in range(4):
        loads[n].wait()
    loads[5].start()
    kk = k[...]
    vv = v[...]
    for h in range(nheads):
        cols = slice(h * H, (h + 1) * H)
        st = jnp.where(allowed, nt(kk, q[:, cols]), -1e30)
        m = jnp.max(st, axis=0, keepdims=True)
        e = jnp.exp2((st - m) * (scale * math.log2(math.e)))
        p = e * (1.0 / jnp.sum(e, axis=0, keepdims=True))
        pt[:, cols] = p.astype(BF16)
        gp = nt(vv, g[:, cols])
        delta = jnp.sum(p * gp, axis=0, keepdims=True)
        dst[:, cols] = (p * (gp - delta)).astype(BF16)

    def stacked(ref):
        return jnp.concatenate([ref[:, h * H : (h + 1) * H] for h in range(nheads)], axis=0)

    gk = jnp.dot(dst[...], stacked(q), preferred_element_type=F32) * scale
    both[:, :H] = gk.astype(BF16)
    gkt[...] = gk.T.astype(BF16)

    loads[4].wait()

    @pl.when(c == 0)
    def _():
        for zq in range(4):
            for xh in range(2):
                cols = [((zq * 4 + zr) * 2 + xh) * H for zr in range(4)]
                tiles = swap_pieces([xn[:, i : i + H] for i in cols])
                for xl in range(4):
                    to = ((xh * 4 + xl) * 4 + zq) * H
                    xp[:, to : to + H] = tiles[xl]

    @pl.when(c == 1)
    def _():
        for half in range(2):
            for t in range(8):
                xp[:, (t * 2 + half) * 256 : (t * 2 + half + 1) * 256] = xn[
                    :, (half * 8 + t) * 256 : (half * 8 + t + 1) * 256
                ]

    def weight_terms(t):
        lanes = pl.ds(pl.multiple_of(t * 512, 512), 512)
        res = jnp.dot(gkt[...], xp[:, lanes], preferred_element_type=F32)
        for ch in range(NCH):
            wt[t, ch] = res[:, ch * H : ch * H + H]

    def partials():
        gv = jnp.dot(pt[...], stacked(g), preferred_element_type=F32)
        both[:, H:] = gv.astype(BF16)
        loads[5].wait()
        bb = both[...]

        def partial(yt, core):
            rows = pl.ds(pl.multiple_of((yt * 2 + core) * 512, 512), 512)
            return nt(bb[:, :H], pr[0, rows, :]) + nt(bb[:, H:], pr[1, rows, :])

        for n, dy in enumerate((2, 1, 3, 0)):
            bps[n] = partial((yh + dy) % 4, 1 - c).astype(BF16)
        for n, dy in enumerate((2, 1, 3, 0)):
            bpo[n] = partial((yh + dy) % 4, c)

    def grad_query():
        for h in range(nheads):
            cols = slice(h * H, (h + 1) * H)
            gq_out[:, cols] = (tn(dst[:, cols], kk) * scale).astype(BF16)

    ccopies = [remote(bps.at[n], bpr.at[n], cs.at[n], cr.at[n], partner) for n in range(4)]

    ysrc = (ysend_p, ysend_m)
    yrec = (yr_p, yr_m)
    ycopies = {
        (d, n): remote(ysrc[d].at[n], yrec[d].at[n], ys.at[d, n], yr.at[d, n], along_y(1 - 2 * d))
        for d in range(2)
        for n in range(3)
    }

    def rows_of(d):
        return slice(d * 64, d * 64 + 64)

    def y_swap():
        for cp in ccopies:
            cp.start()

    def y_first():
        ccopies[0].wait_recv()
        for d in range(2):
            r = rows_of(d)
            ysrc[d][0] = (bpo[0, r] + bpr[0, r].astype(F32)).astype(BF16)
            ycopies[d, 0].start()
        for d in range(2):
            ccopies[1 + d].wait_recv()
            r = rows_of(1 - d)
            ysrc[d][1] = (bpo[1 + d, r] + bpr[1 + d, r].astype(F32)).astype(BF16)
            ycopies[d, 1].start()

    def y_second():
        for d in range(2):
            ycopies[d, 0].wait_recv()
            r = rows_of(d)
            ysrc[d][2] = (
                bpo[1 + d, r] + bpr[1 + d, r].astype(F32) + yrec[d][0].astype(F32)
            ).astype(BF16)
            ycopies[d, 2].start()

    def acopy(d, m, ch):
        return remote(
            am.at[d, m, ch], ar.at[d, m, ch], as_.at[d, m, ch], ars.at[d, m, ch], along_a(1 - 2 * d)
        )

    def fcopy(d):
        return remote(fm.at[d], fr.at[d], fs.at[d], frs.at[d], along_a(3 - 6 * d))

    def ring(m, d):
        for ch in range(NCH):
            val = wt[(a + (1 - 2 * d) * (3 - m) + 8) % 8, ch]
            if m:
                acopy(d, m - 1, ch).wait_recv()
                val = val + ar[d, m - 1, ch].astype(F32)
            am[d, m, ch] = val.astype(BF16)
            if m == 2:
                @pl.when(d == ch // 2)
                def _():
                    if ch % 2 == 0:
                        fcopy(ch // 2).wait_recv()
                    am[ch // 2, m, ch] = (val + fr[ch // 2, ch % 2].astype(F32)).astype(BF16)

            acopy(d, m, ch).start()

    low = (7 - a) // 4

    def ring_step(m):
        ring(m, low)
        ring(m, 1 - low)

    def ring_start():
        for step in (3, 5):
            weight_terms((a + step) % 8)
        ring_step(0)
        weight_terms((a + 4) % 8)
        for d in range(2):
            fm[d] = wt[(a + 4) % 8, 2 * d : 2 * d + 2].astype(BF16)
            fcopy(d).start()
        for step in (2, 6, 1, 7, 0):
            weight_terms((a + step) % 8)

    mine = yl * 8 + b

    def scopy(slot):
        n = (slot // 8 - yl + 2) % 2 * 8 + (slot % 8 - b + 8) % 8
        return remote(s2.at[slot], r2.at[n], s2s.at[slot], s2r.at[n], along_b(n))

    def owners():
        for ch in range(NCH):
            for d in range(2):
                acopy(d, 2, ch).wait_recv()
            tot = wt[a, ch] + ar[0, 2, ch].astype(F32) + ar[1, 2, ch].astype(F32)
            tot = tot.T.reshape(4, 32, H)
            fin[ch * 4 : ch * 4 + 4] = tot
            s2[ch * 4 : ch * 4 + 4] = tot.astype(BF16)
            for slot in range(ch * 4, ch * 4 + 4):
                pl.when(mine != slot)(lambda slot=slot: scopy(slot).start())

    @pl.when(z < 4)
    def _():
        partials()
        grad_query()

    pl.semaphore_wait(barrier, len(peers))
    ring_start()

    @pl.when(z < 4)
    def _():
        y_swap()
        y_first()
        ring_step(1)
        ring_step(2)
        y_second()
        owners()

    @pl.when(z >= 4)
    def _():
        partials()
        y_swap()
        ring_step(1)
        ring_step(2)
        y_first()
        owners()
        grad_query()
        y_second()

    ccopies[3].wait_recv()
    for d in range(2):
        for n in (1, 2):
            ycopies[d, n].wait_recv()
    for r in range(2):
        rr = rows_of(r)
        acc = bpo[3, rr] + bpr[3, rr].astype(F32)
        for d in range(2):
            acc = acc + yrec[d][2 if r == d else 1].astype(F32)
        gi_out[rr, :] = acc.astype(BF16)

    own = fin[mine]
    for n in range(1, 16):
        remote(s2.at[0], r2.at[n], s2s.at[0], s2r.at[n], along_b(n)).wait_recv()
    for n in range(1, 16):
        own = own + r2[n].astype(F32)
    gw_out[...] = own * (1.0 / (2 * 8 * 8))

    for cp in ccopies + list(ycopies.values()):
        cp.wait_send()
    for d in range(2):
        fcopy(d).wait_send()
        for m in range(3):
            for ch in range(NCH):
                acopy(d, m, ch).wait_send()
    for slot in range(16):
        pl.when(mine != slot)(lambda slot=slot: scopy(slot).wait_send())


def put_out(*refs):
    n = len(refs) // 2
    sem = refs[-1]
    copies = [
        pltpu.make_async_copy(src, dst_, sem.at[i])
        for i, (src, dst_) in enumerate(zip(refs[:n], refs[n : 2 * n]))
    ]
    for cp in copies:
        cp.start()
    for cp in copies:
        cp.wait()


def body(query_states, key_states, value_states, grad_context, inputs_normed, projections):
    t, qw = query_states.shape
    d = inputs_normed.shape[1]
    hbm = pl.BlockSpec(memory_space=pl.ANY)
    vmem = pl.BlockSpec(memory_space=pltpu.VMEM)
    V = pltpu.VMEM
    S = pltpu.SemaphoreType.DMA
    shapes = (
        jax.ShapeDtypeStruct((t, qw), BF16),
        jax.ShapeDtypeStruct((t, d // 8), BF16),
        jax.ShapeDtypeStruct((d // 128, H), F32),
    )
    outs = pl.pallas_call(
        kernel,
        out_shape=tuple(V(s.shape, s.dtype) for s in shapes),
        in_specs=[hbm] * 6,
        out_specs=(vmem,) * 3,
        scratch_shapes=[
            V((t, qw), BF16), V((t, H), BF16), V((t, H), BF16), V((t, qw), BF16),
            V((t, d), BF16), V((t, d), BF16), V((2, d, H), BF16),
            V((t, qw), BF16), V((t, qw), BF16), V((H, t), BF16), V((t, 2 * H), BF16),
            V((8, NCH, H, H), F32),
            V((2, 3, NCH, H, H), BF16), V((2, 3, NCH, H, H), BF16),
            V((2, 2, H, H), BF16), V((2, 2, H, H), BF16),
            V((16, 32, H), F32), V((16, 32, H), BF16), V((16, 32, H), BF16),
            V((4, t, 512), F32), V((4, t, 512), BF16), V((4, t, 512), BF16),
            V((3, t // 2, 512), BF16), V((3, t // 2, 512), BF16),
            V((3, t // 2, 512), BF16), V((3, t // 2, 512), BF16),
            S((6,)), S((2, 3, NCH)), S((2, 3, NCH)), S((2,)), S((2,)),
            S((16,)), S((16,)), S((4,)), S((4,)), S((2, 3)), S((2, 3)),
        ],
        compiler_params=pltpu.CompilerParams(collective_id=0, has_side_effects=True),
    )(query_states, key_states, value_states, grad_context, inputs_normed, projections)
    return pl.pallas_call(
        put_out,
        out_shape=shapes,
        in_specs=(vmem,) * 3,
        out_specs=(hbm,) * 3,
        scratch_shapes=[S((3,))],
    )(*[pltpu.with_memory_space_constraint(o, pltpu.VMEM) for o in outs])


def solution(mesh):
    torus = Mesh(mesh.devices.reshape(2, 8, 8, 4, 2), DP + MP)
    return jax.shard_map(
        body,
        mesh=torus,
        in_specs=(P(DP, MP), P(DP, MP), P(DP, MP), P(DP, MP), P(DP, None), P(None, None, MP)),
        out_specs=(P(DP, MP), P(DP, MP), P(DP, MP)),
        check_vma=False,
    )
```

```python
import math

import jax
import jax.numpy as jnp
from jax import lax
from jax.experimental import pallas as pl
from jax.experimental.pallas import tpu as pltpu
from jax.sharding import Mesh
from jax.sharding import PartitionSpec as P

MESH = pl.DeviceIdType.MESH
H = 128
DP = ("yl", "z", "x")
MP = ("yh", "c")
F32 = jnp.float32
BF16 = jnp.bfloat16


def nt(a, b):
    return lax.dot_general(a, b, (((1,), (1,)), ((), ())), preferred_element_type=F32)


def tn(a, b):
    return lax.dot_general(a, b, (((0,), (0,)), ((), ())), preferred_element_type=F32)


NCH = 4
EARLY = 2


def swap_pieces(tiles):
    place = lax.broadcasted_iota(jnp.int32, tiles[0].shape, 1) // 32
    turned = [tiles[0]] + [pltpu.roll(tiles[j], 32 * j, 1) for j in range(1, 4)]
    out = []
    for i in range(4):
        mixed = turned[0]
        for j in range(1, 4):
            mixed = jnp.where(place == (i + j) % 4, turned[j], mixed)
        out.append(pltpu.roll(mixed, H - 32 * i, 1) if i else mixed)
    return out


def kernel(
    q_hbm, k_hbm, v_hbm, g_hbm, xn_hbm, pr_hbm,
    gq_out, gi_out, gw_out,
    q, k, v, g, xn, xp, pr, pt, dst, gkt, both,
    wt, am, ar, fm, fr, fin, s2, r2,
    we, em, er, efm, ef, s2e, own_,
    bpo, bps, bpr, ysend_p, ysend_m, yr_p, yr_m,
    lsem, as_, ars, fs, frs, es, ers, efs, efr, s2es, s2s, s2r, cs, cr, ys, yr,
):
    yl = lax.axis_index("yl")
    z = lax.axis_index("z")
    x = lax.axis_index("x")
    yh = lax.axis_index("yh")
    c = lax.axis_index("c")
    nheads = q.shape[1] // H
    scale = 1.0 / math.sqrt(H)

    loads = [
        pltpu.make_async_copy(src, dst_, lsem.at[n])
        for n, (src, dst_) in enumerate(
            [(k_hbm, k), (q_hbm, q), (v_hbm, v), (g_hbm, g), (xn_hbm, xn), (pr_hbm, pr)]
        )
    ]
    for cp in loads[:5]:
        cp.start()

    def along_y(step):
        return {"yh": (yh + step + 4) % 4}

    a = x + c * (z - x)
    b = z + c * (x - z)

    def along_a(step):
        return {"x": (x + (1 - c) * step + 8) % 8, "z": (z + c * step + 8) % 8}

    def along_b(n):
        return {"x": (x + c * (n % 8)) % 8, "z": (z + (1 - c) * (n % 8)) % 8, "yl": (yl + n // 8) % 2}

    partner = {"c": 1 - c}
    peers = [partner, along_y(1), along_y(-1)]
    peers += [along_b(n) for n in range(1, 16)]
    peers += [{**along_a(n % 8), "yl": (yl + n // 8) % 2} for n in range(1, 16) if n != 8]
    barrier = pltpu.get_barrier_semaphore()
    for peer in peers:
        pl.semaphore_signal(barrier, inc=1, device_id=peer, device_id_type=MESH)

    def remote(src, dst_, ssem, rsem, device):
        return pltpu.make_async_remote_copy(
            src_ref=src, dst_ref=dst_, send_sem=ssem, recv_sem=rsem,
            device_id=device, device_id_type=MESH,
        )

    jpos = lax.broadcasted_iota(jnp.int32, (H, H), 0)
    ipos = lax.broadcasted_iota(jnp.int32, (H, H), 1)
    allowed = jpos <= ipos
    for n in range(4):
        loads[n].wait()
    loads[5].start()
    kk = k[...]
    vv = v[...]
    for h in range(nheads):
        cols = slice(h * H, (h + 1) * H)
        st = jnp.where(allowed, nt(kk, q[:, cols]), -1e30)
        m = jnp.max(st, axis=0, keepdims=True)
        e = jnp.exp2((st - m) * (scale * math.log2(math.e)))
        p = e * (1.0 / jnp.sum(e, axis=0, keepdims=True))
        pt[:, cols] = p.astype(BF16)
        gp = nt(vv, g[:, cols])
        delta = jnp.sum(p * gp, axis=0, keepdims=True)
        dst[:, cols] = (p * (gp - delta)).astype(BF16)

    def stacked(ref):
        return jnp.concatenate([ref[:, h * H : (h + 1) * H] for h in range(nheads)], axis=0)

    gk = jnp.dot(dst[...], stacked(q), preferred_element_type=F32) * scale
    both[:, :H] = gk.astype(BF16)
    gkt[...] = gk.T.astype(BF16)

    def permute():
        @pl.when(c == 0)
        def _():
            for zq in range(4):
                for xh in range(2):
                    cols = [((zq * 4 + zr) * 2 + xh) * H for zr in range(4)]
                    tiles = swap_pieces([xn[:, i : i + H] for i in cols])
                    for xl in range(4):
                        to = ((xh * 4 + xl) * 4 + zq) * H
                        xp[:, to : to + H] = tiles[xl]

        @pl.when(c == 1)
        def _():
            for half in range(2):
                for t in range(8):
                    xp[:, (t * 2 + half) * 256 : (t * 2 + half + 1) * 256] = xn[
                        :, (half * 8 + t) * 256 : (half * 8 + t + 1) * 256
                    ]

    def weight_terms(t):
        lanes = pl.ds(pl.multiple_of(t * 512, 512), 512)
        res = jnp.dot(gkt[...], xp[:, lanes], preferred_element_type=F32)
        for ch in range(NCH):
            wt[t, ch] = res[:, ch * H : ch * H + H]

    def partials():
        gv = jnp.dot(pt[...], stacked(g), preferred_element_type=F32)
        both[:, H:] = gv.astype(BF16)
        loads[5].wait()
        bb = both[...]

        def partial(yt, core):
            rows = pl.ds(pl.multiple_of((yt * 2 + core) * 512, 512), 512)
            return nt(bb[:, :H], pr[0, rows, :]) + nt(bb[:, H:], pr[1, rows, :])

        for n, dy in enumerate((2, 1, 3, 0)):
            bps[n] = partial((yh + dy) % 4, 1 - c).astype(BF16)
        for n, dy in enumerate((2, 1, 3, 0)):
            bpo[n] = partial((yh + dy) % 4, c)

    def grad_query():
        for h in range(nheads):
            cols = slice(h * H, (h + 1) * H)
            gq_out[:, cols] = (tn(dst[:, cols], kk) * scale).astype(BF16)

    ccopies = [remote(bps.at[n], bpr.at[n], cs.at[n], cr.at[n], partner) for n in range(4)]

    ysrc = (ysend_p, ysend_m)
    yrec = (yr_p, yr_m)
    ycopies = {
        (d, n): remote(ysrc[d].at[n], yrec[d].at[n], ys.at[d, n], yr.at[d, n], along_y(1 - 2 * d))
        for d in range(2)
        for n in range(3)
    }

    def rows_of(d):
        return slice(d * 64, d * 64 + 64)

    def y_swap():
        for cp in ccopies:
            cp.start()

    def y_first():
        ccopies[0].wait_recv()
        for d in range(2):
            r = rows_of(d)
            ysrc[d][0] = (bpo[0, r] + bpr[0, r].astype(F32)).astype(BF16)
            ycopies[d, 0].start()
        for d in range(2):
            ccopies[1 + d].wait_recv()
            r = rows_of(1 - d)
            ysrc[d][1] = (bpo[1 + d, r] + bpr[1 + d, r].astype(F32)).astype(BF16)
            ycopies[d, 1].start()

    def y_second():
        for d in range(2):
            ycopies[d, 0].wait_recv()
            r = rows_of(d)
            ysrc[d][2] = (
                bpo[1 + d, r] + bpr[1 + d, r].astype(F32) + yrec[d][0].astype(F32)
            ).astype(BF16)
            ycopies[d, 2].start()

    def acopy(d, m, ch):
        return remote(
            am.at[d, m, ch], ar.at[d, m, ch], as_.at[d, m, ch], ars.at[d, m, ch], along_a(1 - 2 * d)
        )

    def fcopy(d):
        return remote(fm.at[d], fr.at[d], fs.at[d], frs.at[d], along_a(3 - 6 * d))

    def ring(m, d):
        for ch in range(NCH):
            val = wt[(a + (1 - 2 * d) * (3 - m) + 8) % 8, ch]
            if m:
                acopy(d, m - 1, ch).wait_recv()
                val = val + ar[d, m - 1, ch].astype(F32)
            am[d, m, ch] = val.astype(BF16)
            if m == 2:
                @pl.when(d == ch // 2)
                def _():
                    if ch % 2 == 0:
                        fcopy(ch // 2).wait_recv()
                    am[ch // 2, m, ch] = (val + fr[ch // 2, ch % 2].astype(F32)).astype(BF16)

            acopy(d, m, ch).start()

    low = (7 - a) // 4

    def ring_step(m):
        ring(m, low)
        ring(m, 1 - low)

    def ring_start():
        for step in (3, 5):
            weight_terms((a + step) % 8)
        ring_step(0)
        weight_terms((a + 4) % 8)
        for d in range(2):
            fm[d] = wt[(a + 4) % 8, 2 * d : 2 * d + 2].astype(BF16)
            fcopy(d).start()
        for step in (2, 6, 1, 7, 0):
            weight_terms((a + step) % 8)

    def early_terms():
        for t in range(EARLY):
            for half in range(2):
                lanes = slice((half * 8 + t) * 256, (half * 8 + t + 1) * 256)
                res = jnp.dot(gkt[...], xn[:, lanes], preferred_element_type=F32)
                for xh in range(2):
                    we[t, half * 2 + xh] = res[:, xh * H : xh * H + H]

    def at(t, r):
        return jnp.logical_and(c == 0, (z - t + 8) % 8 == r)

    def ecopy(t, r, ch):
        d = 1 if r < 4 else 0
        return remote(
            em.at[t, ch], er.at[t, d, ch], es.at[t, ch], ers.at[t, d, ch], {"z": (z + 1 - 2 * d + 8) % 8}
        )

    def efcopy(t, d):
        return remote(efm.at[t, d], ef.at[t], efs.at[t, d], efr.at[t], {"z": (z + 3 - 6 * d + 8) % 8})

    def early_far(t):
        for d in range(2):
            efm[t, d] = we[t, 2 * d : 2 * d + 2].astype(BF16)
            efcopy(t, d).start()

    def early_chain(t, r):
        d = 1 if r < 4 else 0
        for ch in range(NCH):
            val = we[t, ch]
            if r not in (3, 5):
                ecopy(t, r, ch).wait_recv()
                val = val + er[t, d, ch].astype(F32)
            if r in (1, 7) and ch // 2 == d:
                if ch % 2 == 0:
                    efcopy(t, d).wait_recv()
                val = val + ef[t, ch % 2].astype(F32)
            em[t, ch] = val.astype(BF16)
            ecopy(t, r, ch).start()

    def early(*rs):
        for t in range(EARLY):
            for r in rs:
                if r == 4:
                    pl.when(at(t, r))(lambda t=t: early_far(t))
                else:
                    pl.when(at(t, r))(lambda t=t, r=r: early_chain(t, r))

    def escopy(slot):
        n = (slot // 8 - yl + 2) % 2 * 8 + (slot % 8 - x + 8) % 8
        return remote(
            s2e.at[slot], r2.at[n], s2es.at[slot], s2r.at[n], {"x": (x + n % 8) % 8, "yl": (yl + n // 8) % 2}
        )

    own_early = jnp.logical_and(c == 0, z < EARLY)

    def early_owner(t):
        for ch in range(NCH):
            for d in range(2):
                ecopy(t, 1 if d else 7, ch).wait_recv()
            tot = we[t, ch] + er[t, 0, ch].astype(F32) + er[t, 1, ch].astype(F32)
            tot = tot.T.reshape(4, 32, H)
            s2e[ch * 4 : ch * 4 + 4] = tot.astype(BF16)
            for i in range(4):
                slot = ch * 4 + i
                pl.when(yl * 8 + x == slot)(lambda tot=tot, i=i: own_.__setitem__(..., tot[i]))
                pl.when(yl * 8 + x != slot)(lambda slot=slot: escopy(slot).start())

    def early_owners():
        for t in range(EARLY):
            pl.when(at(t, 0))(lambda t=t: early_owner(t))

    mine = yl * 8 + b

    def scopy(slot):
        n = (slot // 8 - yl + 2) % 2 * 8 + (slot % 8 - b + 8) % 8
        return remote(s2.at[slot], r2.at[n], s2s.at[slot], s2r.at[n], along_b(n))

    def sends(slot):
        if slot % 8 < EARLY:
            return jnp.logical_and(c == 1, mine != slot)
        return mine != slot

    def owners():
        for ch in range(NCH):
            for d in range(2):
                acopy(d, 2, ch).wait_recv()
            tot = wt[a, ch] + ar[0, 2, ch].astype(F32) + ar[1, 2, ch].astype(F32)
            tot = tot.T.reshape(4, 32, H)
            fin[ch * 4 : ch * 4 + 4] = tot
            s2[ch * 4 : ch * 4 + 4] = tot.astype(BF16)
            for slot in range(ch * 4, ch * 4 + 4):
                pl.when(sends(slot))(lambda slot=slot: scopy(slot).start())

    loads[4].wait()
    pl.when(c == 0)(early_terms)

    @pl.when(z < 4)
    def _():
        partials()
        grad_query()

    pl.semaphore_wait(barrier, len(peers))
    early(5, 3, 4)
    permute()
    ring_start()

    @pl.when(z < 4)
    def _():
        y_swap()
        y_first()
        early(2)
        ring_step(1)
        early(1)
        ring_step(2)
        early(7)
        y_second()
        owners()
        early_owners()

    @pl.when(z >= 4)
    def _():
        early(6)
        partials()
        y_swap()
        ring_step(1)
        early(7)
        ring_step(2)
        y_first()
        owners()
        grad_query()
        y_second()

    ccopies[3].wait_recv()
    for d in range(2):
        for n in (1, 2):
            ycopies[d, n].wait_recv()
    for r in range(2):
        rr = rows_of(r)
        acc = bpo[3, rr] + bpr[3, rr].astype(F32)
        for d in range(2):
            acc = acc + yrec[d][2 if r == d else 1].astype(F32)
        gi_out[rr, :] = acc.astype(BF16)

    @pl.when(jnp.logical_not(own_early))
    def _():
        own_[...] = fin[mine]

    own = own_[...]
    for n in range(1, 16):
        remote(s2.at[0], r2.at[n], s2s.at[0], s2r.at[n], along_b(n)).wait_recv()
    for n in range(1, 16):
        own = own + r2[n].astype(F32)
    gw_out[...] = own * (1.0 / (2 * 8 * 8))

    for cp in ccopies + list(ycopies.values()):
        cp.wait_send()
    for d in range(2):
        fcopy(d).wait_send()
        for m in range(3):
            for ch in range(NCH):
                acopy(d, m, ch).wait_send()
    for slot in range(16):
        pl.when(sends(slot))(lambda slot=slot: scopy(slot).wait_send())
        pl.when(jnp.logical_and(own_early, yl * 8 + x != slot))(lambda slot=slot: escopy(slot).wait_send())
    for t in range(EARLY):
        for ch in range(NCH):
            pl.when(jnp.logical_and(c == 0, (z - t + 8) % 4 != 0))(lambda t=t, ch=ch: ecopy(t, 1, ch).wait_send())
        for d in range(2):
            pl.when(at(t, 4))(lambda t=t, d=d: efcopy(t, d).wait_send())


def put_out(*refs):
    n = len(refs) // 2
    sem = refs[-1]
    copies = [
        pltpu.make_async_copy(src, dst_, sem.at[i])
        for i, (src, dst_) in enumerate(zip(refs[:n], refs[n : 2 * n]))
    ]
    for cp in copies:
        cp.start()
    for cp in copies:
        cp.wait()


def body(query_states, key_states, value_states, grad_context, inputs_normed, projections):
    t, qw = query_states.shape
    d = inputs_normed.shape[1]
    hbm = pl.BlockSpec(memory_space=pl.ANY)
    vmem = pl.BlockSpec(memory_space=pltpu.VMEM)
    V = pltpu.VMEM
    S = pltpu.SemaphoreType.DMA
    shapes = (
        jax.ShapeDtypeStruct((t, qw), BF16),
        jax.ShapeDtypeStruct((t, d // 8), BF16),
        jax.ShapeDtypeStruct((d // 128, H), F32),
    )
    outs = pl.pallas_call(
        kernel,
        out_shape=tuple(V(s.shape, s.dtype) for s in shapes),
        in_specs=[hbm] * 6,
        out_specs=(vmem,) * 3,
        scratch_shapes=[
            V((t, qw), BF16), V((t, H), BF16), V((t, H), BF16), V((t, qw), BF16),
            V((t, d), BF16), V((t, d), BF16), V((2, d, H), BF16),
            V((t, qw), BF16), V((t, qw), BF16), V((H, t), BF16), V((t, 2 * H), BF16),
            V((8, NCH, H, H), F32),
            V((2, 3, NCH, H, H), BF16), V((2, 3, NCH, H, H), BF16),
            V((2, 2, H, H), BF16), V((2, 2, H, H), BF16),
            V((16, 32, H), F32), V((16, 32, H), BF16), V((16, 32, H), BF16),
            V((EARLY, NCH, H, H), F32), V((EARLY, NCH, H, H), BF16), V((EARLY, 2, NCH, H, H), BF16),
            V((EARLY, 2, 2, H, H), BF16), V((EARLY, 2, H, H), BF16), V((16, 32, H), BF16), V((32, H), F32),
            V((4, t, 512), F32), V((4, t, 512), BF16), V((4, t, 512), BF16),
            V((3, t // 2, 512), BF16), V((3, t // 2, 512), BF16),
            V((3, t // 2, 512), BF16), V((3, t // 2, 512), BF16),
            S((6,)), S((2, 3, NCH)), S((2, 3, NCH)), S((2,)), S((2,)),
            S((EARLY, NCH)), S((EARLY, 2, NCH)), S((EARLY, 2)), S((EARLY,)), S((16,)),
            S((16,)), S((16,)), S((4,)), S((4,)), S((2, 3)), S((2, 3)),
        ],
        compiler_params=pltpu.CompilerParams(collective_id=0, has_side_effects=True),
    )(query_states, key_states, value_states, grad_context, inputs_normed, projections)
    return pl.pallas_call(
        put_out,
        out_shape=shapes,
        in_specs=(vmem,) * 3,
        out_specs=(hbm,) * 3,
        scratch_shapes=[S((3,))],
    )(*[pltpu.with_memory_space_constraint(o, pltpu.VMEM) for o in outs])


def solution(mesh):
    torus = Mesh(mesh.devices.reshape(2, 8, 8, 4, 2), DP + MP)
    return jax.shard_map(
        body,
        mesh=torus,
        in_specs=(P(DP, MP), P(DP, MP), P(DP, MP), P(DP, MP), P(DP, None), P(None, None, MP)),
        out_specs=(P(DP, MP), P(DP, MP), P(DP, MP)),
        check_vma=False,
    )
```

```python
import math

import jax
import jax.numpy as jnp
from jax import lax
from jax.experimental import pallas as pl
from jax.experimental.pallas import tpu as pltpu
from jax.sharding import Mesh
from jax.sharding import PartitionSpec as P

MESH = pl.DeviceIdType.MESH
H = 128
DP = ("yl", "z", "x")
MP = ("yh", "c")
F32 = jnp.float32
BF16 = jnp.bfloat16


def nt(a, b):
    return lax.dot_general(a, b, (((1,), (1,)), ((), ())), preferred_element_type=F32)


def tn(a, b):
    return lax.dot_general(a, b, (((0,), (0,)), ((), ())), preferred_element_type=F32)


NCH = 4


def swap_pieces(tiles):
    place = lax.broadcasted_iota(jnp.int32, tiles[0].shape, 1) // 32
    turned = [tiles[0]] + [pltpu.roll(tiles[j], 32 * j, 1) for j in range(1, 4)]
    out = []
    for i in range(4):
        mixed = turned[0]
        for j in range(1, 4):
            mixed = jnp.where(place == (i + j) % 4, turned[j], mixed)
        out.append(pltpu.roll(mixed, H - 32 * i, 1) if i else mixed)
    return out


def kernel(
    q_hbm, k_hbm, v_hbm, g_hbm, xn_hbm, pr_hbm,
    gq_out, gi_out, gw_out,
    q, k, v, g, xn, xp, pr, pt, dst, gkt, both,
    wt, am, ar, fm, fr, fin, s2, r2,
    bpo, bps, bpr, ysend_p, ysend_m, yr_p, yr_m,
    lsem, as_, ars, fs, frs, s2s, s2r, cs, cr, ys, yr,
):
    yl = lax.axis_index("yl")
    z = lax.axis_index("z")
    x = lax.axis_index("x")
    yh = lax.axis_index("yh")
    c = lax.axis_index("c")
    nheads = q.shape[1] // H
    scale = 1.0 / math.sqrt(H)

    loads = [
        pltpu.make_async_copy(src, dst_, lsem.at[n])
        for n, (src, dst_) in enumerate(
            [(k_hbm, k), (q_hbm, q), (v_hbm, v), (g_hbm, g), (xn_hbm, xn), (pr_hbm, pr)]
        )
    ]
    for cp in loads[:5]:
        cp.start()

    def along_y(step):
        return {"yh": (yh + step + 4) % 4}

    a = x + c * (z - x)
    b = z + c * (x - z)

    def along_a(step):
        return {"x": (x + (1 - c) * step + 8) % 8, "z": (z + c * step + 8) % 8}

    def along_b(n):
        return {"x": (x + c * (n % 8)) % 8, "z": (z + (1 - c) * (n % 8)) % 8, "yl": (yl + n // 8) % 2}

    partner = {"c": 1 - c}
    peers = [partner, along_y(1), along_y(-1)]
    peers += [along_a(n) for n in (1, -1, 3, -3)]
    peers += [along_b(n) for n in range(1, 16)]
    barrier = pltpu.get_barrier_semaphore()
    for peer in peers:
        pl.semaphore_signal(barrier, inc=1, device_id=peer, device_id_type=MESH)

    def remote(src, dst_, ssem, rsem, device):
        return pltpu.make_async_remote_copy(
            src_ref=src, dst_ref=dst_, send_sem=ssem, recv_sem=rsem,
            device_id=device, device_id_type=MESH,
        )

    jpos = lax.broadcasted_iota(jnp.int32, (H, H), 0)
    ipos = lax.broadcasted_iota(jnp.int32, (H, H), 1)
    allowed = jpos <= ipos
    for n in range(4):
        loads[n].wait()
    loads[5].start()
    kk = k[...]
    vv = v[...]
    for h in range(nheads):
        cols = slice(h * H, (h + 1) * H)
        st = jnp.where(allowed, nt(kk, q[:, cols]), -1e30)
        m = jnp.max(st, axis=0, keepdims=True)
        e = jnp.exp2((st - m) * (scale * math.log2(math.e)))
        p = e * (1.0 / jnp.sum(e, axis=0, keepdims=True))
        pt[:, cols] = p.astype(BF16)
        gp = nt(vv, g[:, cols])
        delta = jnp.sum(p * gp, axis=0, keepdims=True)
        dst[:, cols] = (p * (gp - delta)).astype(BF16)

    def stacked(ref):
        return jnp.concatenate([ref[:, h * H : (h + 1) * H] for h in range(nheads)], axis=0)

    gk = jnp.dot(dst[...], stacked(q), preferred_element_type=F32) * scale
    both[:, :H] = gk.astype(BF16)
    gkt[...] = gk.T.astype(BF16)

    loads[4].wait()

    @pl.when(c == 0)
    def _():
        for zq in range(4):
            for xh in range(2):
                cols = [((zq * 4 + zr) * 2 + xh) * H for zr in range(4)]
                tiles = swap_pieces([xn[:, i : i + H] for i in cols])
                for xl in range(4):
                    to = ((xh * 4 + xl) * 4 + zq) * H
                    xp[:, to : to + H] = tiles[xl]

    @pl.when(c == 1)
    def _():
        for half in range(2):
            for t in range(8):
                xp[:, (t * 2 + half) * 256 : (t * 2 + half + 1) * 256] = xn[
                    :, (half * 8 + t) * 256 : (half * 8 + t + 1) * 256
                ]

    def weight_terms(t):
        lanes = pl.ds(pl.multiple_of(t * 512, 512), 512)
        res = jnp.dot(gkt[...], xp[:, lanes], preferred_element_type=F32)
        for ch in range(NCH):
            wt[t, ch] = res[:, ch * H : ch * H + H]

    def partials():
        gv = jnp.dot(pt[...], stacked(g), preferred_element_type=F32)
        both[:, H:] = gv.astype(BF16)
        loads[5].wait()
        bb = both[...]

        def partial(yt, core):
            rows = pl.ds(pl.multiple_of((yt * 2 + core) * 512, 512), 512)
            return nt(bb[:, :H], pr[0, rows, :]) + nt(bb[:, H:], pr[1, rows, :])

        for n, dy in enumerate((2, 1, 3, 0)):
            bps[n] = partial((yh + dy) % 4, 1 - c).astype(BF16)
        for n, dy in enumerate((2, 1, 3, 0)):
            bpo[n] = partial((yh + dy) % 4, c)

    def grad_query():
        for h in range(nheads):
            cols = slice(h * H, (h + 1) * H)
            gq_out[:, cols] = (tn(dst[:, cols], kk) * scale).astype(BF16)

    ccopies = [remote(bps.at[n], bpr.at[n], cs.at[n], cr.at[n], partner) for n in range(4)]

    ysrc = (ysend_p, ysend_m)
    yrec = (yr_p, yr_m)
    ycopies = {
        (d, n): remote(ysrc[d].at[n], yrec[d].at[n], ys.at[d, n], yr.at[d, n], along_y(1 - 2 * d))
        for d in range(2)
        for n in range(3)
    }

    def rows_of(d):
        return slice(d * 64, d * 64 + 64)

    def y_swap():
        for cp in ccopies:
            cp.start()

    def y_first():
        ccopies[0].wait_recv()
        for d in range(2):
            r = rows_of(d)
            ysrc[d][0] = (bpo[0, r] + bpr[0, r].astype(F32)).astype(BF16)
            ycopies[d, 0].start()
        for d in range(2):
            ccopies[1 + d].wait_recv()
            r = rows_of(1 - d)
            ysrc[d][1] = (bpo[1 + d, r] + bpr[1 + d, r].astype(F32)).astype(BF16)
            ycopies[d, 1].start()

    def y_second():
        for d in range(2):
            ycopies[d, 0].wait_recv()
            r = rows_of(d)
            ysrc[d][2] = (
                bpo[1 + d, r] + bpr[1 + d, r].astype(F32) + yrec[d][0].astype(F32)
            ).astype(BF16)
            ycopies[d, 2].start()

    def acopy(d, m, ch):
        return remote(
            am.at[d, m, ch], ar.at[d, m, ch], as_.at[d, m, ch], ars.at[d, m, ch], along_a(1 - 2 * d)
        )

    def fcopy(d, i):
        return remote(fm.at[d, i], fr.at[d, i], fs.at[d, i], frs.at[d, i], along_a(3 - 6 * d))

    def ring(m, d, wave):
        for ch in (wave, wave + 2):
            val = wt[(a + (1 - 2 * d) * (3 - m) + 8) % 8, ch]
            if m:
                acopy(d, m - 1, ch).wait_recv()
                val = val + ar[d, m - 1, ch].astype(F32)
            am[d, m, ch] = val.astype(BF16)
            if m == 2:
                @pl.when(d == ch // 2)
                def _():
                    fcopy(ch // 2, wave).wait_recv()
                    am[ch // 2, m, ch] = (val + fr[ch // 2, wave].astype(F32)).astype(BF16)

            acopy(d, m, ch).start()

    low = c * ((7 - a) // 4) + (1 - c) * (a // 4)

    def ring_step(m, wave):
        ring(m, low, wave)
        ring(m, 1 - low, wave)

    def start_wave(wave):
        ring_step(0, wave)
        for d in range(2):
            fm[d, wave] = wt[(a + 4) % 8, 2 * d + wave].astype(BF16)
            fcopy(d, wave).start()

    def ring_start():
        for step in (3, 5, 4):
            weight_terms((a + step) % 8)
        start_wave(0)
        for step in (2, 6, 1, 7, 0):
            weight_terms((a + step) % 8)

    def ring_middle():
        ring_step(1, 0)
        start_wave(1)
        ring_step(2, 0)
        ring_step(1, 1)

    def ring_end():
        owners(0)
        ring_step(2, 1)
        owners(1)

    mine = yl * 8 + b

    def scopy(slot):
        n = (slot // 8 - yl + 2) % 2 * 8 + (slot % 8 - b + 8) % 8
        return remote(s2.at[slot], r2.at[n], s2s.at[slot], s2r.at[n], along_b(n))

    def owners(wave):
        for ch in (wave, wave + 2):
            for d in range(2):
                acopy(d, 2, ch).wait_recv()
            tot = wt[a, ch] + ar[0, 2, ch].astype(F32) + ar[1, 2, ch].astype(F32)
            tot = tot.T.reshape(4, 32, H)
            fin[ch * 4 : ch * 4 + 4] = tot
            s2[ch * 4 : ch * 4 + 4] = tot.astype(BF16)
            for slot in range(ch * 4, ch * 4 + 4):
                pl.when(mine != slot)(lambda slot=slot: scopy(slot).start())

    @pl.when(z < 4)
    def _():
        partials()
        grad_query()

    pl.semaphore_wait(barrier, len(peers))
    ring_start()

    @pl.when(z < 4)
    def _():
        y_swap()
        y_first()
        ring_middle()
        y_second()
        ring_end()

    @pl.when(jnp.logical_and(z >= 4, z < 6))
    def _():
        partials()
        y_swap()
        ring_middle()
        y_first()
        ring_end()
        grad_query()
        y_second()

    @pl.when(z >= 6)
    def _():
        ring_middle()
        owners(0)
        partials()
        y_swap()
        ring_step(2, 1)
        owners(1)
        y_first()
        grad_query()
        y_second()

    ccopies[3].wait_recv()
    for d in range(2):
        for n in (1, 2):
            ycopies[d, n].wait_recv()
    for r in range(2):
        rr = rows_of(r)
        acc = bpo[3, rr] + bpr[3, rr].astype(F32)
        for d in range(2):
            acc = acc + yrec[d][2 if r == d else 1].astype(F32)
        gi_out[rr, :] = acc.astype(BF16)

    own = fin[mine]
    for n in range(1, 16):
        remote(s2.at[0], r2.at[n], s2s.at[0], s2r.at[n], along_b(n)).wait_recv()
    for n in range(1, 16):
        own = own + r2[n].astype(F32)
    gw_out[...] = own * (1.0 / (2 * 8 * 8))

    for cp in ccopies + list(ycopies.values()):
        cp.wait_send()
    for d in range(2):
        for i in range(2):
            fcopy(d, i).wait_send()
        for m in range(3):
            for ch in range(NCH):
                acopy(d, m, ch).wait_send()
    for slot in range(16):
        pl.when(mine != slot)(lambda slot=slot: scopy(slot).wait_send())


def put_out(*refs):
    n = len(refs) // 2
    sem = refs[-1]
    copies = [
        pltpu.make_async_copy(src, dst_, sem.at[i])
        for i, (src, dst_) in enumerate(zip(refs[:n], refs[n : 2 * n]))
    ]
    for cp in copies:
        cp.start()
    for cp in copies:
        cp.wait()


def body(query_states, key_states, value_states, grad_context, inputs_normed, projections):
    t, qw = query_states.shape
    d = inputs_normed.shape[1]
    hbm = pl.BlockSpec(memory_space=pl.ANY)
    vmem = pl.BlockSpec(memory_space=pltpu.VMEM)
    V = pltpu.VMEM
    S = pltpu.SemaphoreType.DMA
    shapes = (
        jax.ShapeDtypeStruct((t, qw), BF16),
        jax.ShapeDtypeStruct((t, d // 8), BF16),
        jax.ShapeDtypeStruct((d // 128, H), F32),
    )
    outs = pl.pallas_call(
        kernel,
        out_shape=tuple(V(s.shape, s.dtype) for s in shapes),
        in_specs=[hbm] * 6,
        out_specs=(vmem,) * 3,
        scratch_shapes=[
            V((t, qw), BF16), V((t, H), BF16), V((t, H), BF16), V((t, qw), BF16),
            V((t, d), BF16), V((t, d), BF16), V((2, d, H), BF16),
            V((t, qw), BF16), V((t, qw), BF16), V((H, t), BF16), V((t, 2 * H), BF16),
            V((8, NCH, H, H), F32),
            V((2, 3, NCH, H, H), BF16), V((2, 3, NCH, H, H), BF16),
            V((2, 2, H, H), BF16), V((2, 2, H, H), BF16),
            V((16, 32, H), F32), V((16, 32, H), BF16), V((16, 32, H), BF16),
            V((4, t, 512), F32), V((4, t, 512), BF16), V((4, t, 512), BF16),
            V((3, t // 2, 512), BF16), V((3, t // 2, 512), BF16),
            V((3, t // 2, 512), BF16), V((3, t // 2, 512), BF16),
            S((6,)), S((2, 3, NCH)), S((2, 3, NCH)), S((2, 2)), S((2, 2)),
            S((16,)), S((16,)), S((4,)), S((4,)), S((2, 3)), S((2, 3)),
        ],
        compiler_params=pltpu.CompilerParams(collective_id=0, has_side_effects=True),
    )(query_states, key_states, value_states, grad_context, inputs_normed, projections)
    return pl.pallas_call(
        put_out,
        out_shape=shapes,
        in_specs=(vmem,) * 3,
        out_specs=(hbm,) * 3,
        scratch_shapes=[S((3,))],
    )(*[pltpu.with_memory_space_constraint(o, pltpu.VMEM) for o in outs])


def solution(mesh):
    torus = Mesh(mesh.devices.reshape(2, 8, 8, 4, 2), DP + MP)
    return jax.shard_map(
        body,
        mesh=torus,
        in_specs=(P(DP, MP), P(DP, MP), P(DP, MP), P(DP, MP), P(DP, None), P(None, None, MP)),
        out_specs=(P(DP, MP), P(DP, MP), P(DP, MP)),
        check_vma=False,
    )
```
